256 devices in a mesh: expert: 32 (over z, y), tensor: 4 (over x), dp: 2 (over core).
Axes of the slice: x: 4, y: 4, z: 8, core: 2. Of those that a mesh axis runs over, the one named last changes fastest.
Arguments:
- tokens: bfloat16 [1024, 7168], P(('expert', 'dp')), may hold values from -6 to 6
- expert_ids: int32 [1024, 8], P(('expert', 'dp')), may hold values from 0 to 31, all different within a row; in each aligned block of 16 rows (0 to 15, 16 to 31, ...) at most 8 rows name the same one
- route_scores: float32 [1024, 8], P(('expert', 'dp')), may hold values from 0.05 to 1
- gate_weight: bfloat16 [32, 7168, 2048], P('expert', 'dp', 'tensor'), may hold values from -0.0625 to 0.0625
- up_weight: bfloat16 [32, 7168, 2048], P('expert', 'dp', 'tensor'), may hold values from -0.0625 to 0.0625
- down_weight: bfloat16 [32, 2048, 7168], P('expert', 'tensor', 'dp'), may hold values from -0.125 to 0.125
Outputs:
- mixed: bfloat16 [1024, 2, 3584], P(('expert', 'dp'), None, 'tensor')
The draws below stay inside these ranges and needn't reach their ends.
Inputs may be any that keep to these rules, and one draw needn't show every extreme that they name: `expert_ids`: each token names 8 different experts. In each aligned block of 16 tokens (the tokens of one device along expert and dp) no expert is named by more than 8 tokens, a bound that some block reaches.
All inputs are finite; a program needn't handle non-finite values.
Results may differ from the reference program's by a relative error of at most 0.02.
Values may be sent and summed in bfloat16 or wider, within the bound.
A program may use at most 64 MiB of HBM per device.

```python
import math
import jax
import jax.numpy as jnp
import numpy as np
from jax import lax

D = 7168
FF = 2048
TOP = 8
EXPERTS = 32
TOK_DEV = 16
CAP = 8
TOKENS = 1024
N_TENSOR = 4
N_DP = 2


def level_of(rng, shape, split, smallest, high):
    gain, own = 1.0, jax.random.fold_in(rng, 6)
    for dim, blocks in split:
        steps = jnp.exp(jax.random.uniform(jax.random.fold_in(own, dim), (blocks,), jnp.float32, smallest / len(split), high / len(split)))
        gain = gain * jnp.repeat(steps, shape[dim] // blocks).reshape([-1 if axis == dim else 1 for axis in range(len(shape))])
    return gain


def shared_out(key, own, number, rows, number_of, top, bound, slope):
    ranking = jax.random.permutation(key, number_of)
    packed, common = portions_of(number_of, rows * top, bound, slope, True), portions_of(number_of, rows * top, bound, slope, False)
    places = jnp.arange(number_of)

    def named(lengths, turn):
        used = int((lengths > 0).sum())
        fixed = max(1, used // 4)
        moved = fixed + (places - fixed + turn * (used - fixed)) % max(1, number_of - fixed)
        return jnp.zeros((number_of,), jnp.int32).at[ranking[jnp.where(places < fixed, places, moved)]].set(jnp.asarray(lengths, jnp.int32))

    lengths = jnp.where(number % 4 == 0, named(packed, number // 4), named(common, number - number // 4 - 1))
    mixed = jax.random.permutation(jax.random.fold_in(own, 3), number_of)
    source_of, receiver = mixed[0:number_of // 2 * 2:2], mixed[1:number_of // 2 * 2:2]
    slack = jnp.minimum(lengths[source_of] - 1, bound - lengths[receiver]) // 2
    slack = jnp.where((source_of == ranking[0]) | (receiver == ranking[0]) | (lengths[receiver] == 0), 0, jnp.maximum(slack, 0))
    moved = jax.random.randint(jax.random.fold_in(own, 4), (number_of // 2,), 0, 1 << 20) % (slack + 1)
    lengths = lengths.at[source_of].add(-moved).at[receiver].add(moved)
    labels = jnp.searchsorted(jnp.cumsum(lengths), jnp.arange(rows * top), side="right").astype(jnp.int32)
    grid = labels.reshape(top, rows).T
    grid = grid[jax.random.permutation(jax.random.fold_in(own, 1), rows)]
    turn = jax.random.randint(jax.random.fold_in(own, 2), (rows, 1), 0, top)
    return jnp.take_along_axis(grid, (jnp.arange(top)[None, :] + turn) % top, axis=1)


def portions_of(number_of, total, most, lean, full):
    loads = [(1 << 20) // math.isqrt(rank ** lean) + 1 for rank in range(1, number_of + 1)]
    largest = most if full else min(most, max(-(-total // number_of), total * loads[0] // sum(loads)))
    least = 1 if total - largest >= number_of - 1 else 0
    given, surplus = [largest] + [least] * (number_of - 1), total - largest - least * (number_of - 1)
    while surplus > 0:
        free = [i for i in range(1, number_of) if given[i] < largest] or [i for i in range(1, number_of) if given[i] < most]
        pool, budget = sum([loads[i] for i in free]), surplus
        for i in free:
            extra = min(most - given[i], max(1, budget * loads[i] // pool), surplus)
            given[i] = given[i] + extra
            surplus = surplus - extra
    return np.array(given)


def normal_values(stream_key, dims, deviation, bound, shards=(), kind=jnp.bfloat16):
    drawn = deviation * jax.random.normal(stream_key, dims, jnp.float32)
    if shards:
        drawn = drawn * level_of(stream_key, dims, shards, -0.22, 0.18)
    return jnp.clip(drawn, -bound, bound).astype(kind)


def setup_inputs(seed: int = 0) -> dict:
    splits = jax.random.split(jax.random.key(seed), 7)
    tokens = normal_values(splits[0], (TOKENS, D), 1.0, 6.0, ((0, 64),))
    expert_ids_keys = jax.random.split(jax.random.fold_in(splits[1], 1), TOKENS // TOK_DEV)
    expert_ids_turns = jax.random.permutation(jax.random.fold_in(splits[1], 3), TOKENS // TOK_DEV)
    expert_ids = jax.vmap(lambda own, number: shared_out(jax.random.fold_in(splits[1], 2), own, number, TOK_DEV, EXPERTS, TOP, CAP, 2))(expert_ids_keys, expert_ids_turns).reshape((TOKENS, TOP))
    route_scores = jnp.clip(jnp.exp(math.log(1.0) - 2.9957323 * jax.random.uniform(splits[2], (TOKENS, TOP), jnp.float32) ** level_of(splits[2], (TOKENS, TOP), ((0, 64),), -0.2, 0.2)), 0.05, 1.0)
    gate_weight = normal_values(splits[3], (EXPERTS, D, FF), D ** -0.5, 0.0625, ((0, 32), (1, 2), (2, 4)))
    up_weight = normal_values(splits[4], (EXPERTS, D, FF), D ** -0.5, 0.0625, ((0, 32), (1, 2), (2, 4)))
    down_weight = normal_values(splits[5], (EXPERTS, FF, D), FF ** -0.5, 0.125, ((0, 32), (1, 4), (2, 2)))
    return {"tokens": tokens, "expert_ids": expert_ids, "route_scores": route_scores, "gate_weight": gate_weight, "up_weight": up_weight, "down_weight": down_weight}


def reference(tokens, expert_ids, route_scores, gate_weight, up_weight, down_weight):
    groups = TOKENS // TOK_DEV
    pair_ids = expert_ids.reshape(groups, TOK_DEV * TOP)
    expert_hot = (pair_ids[:, :, None] == jnp.arange(EXPERTS, dtype=jnp.int32)[None, None, :]).astype(jnp.int32)
    earlier = jnp.cumsum(expert_hot, axis=1) - expert_hot
    slot_index = jnp.sum(earlier * expert_hot, axis=2).astype(jnp.int32)
    group_index = jnp.arange(groups, dtype=jnp.int32)[:, None]
    target = (pair_ids * (groups * CAP) + group_index * CAP + slot_index).reshape(-1).astype(jnp.int32)
    sources = jnp.repeat(tokens, TOP, axis=0)
    routed = jnp.zeros((EXPERTS * groups * CAP, D), tokens.dtype).at[target].set(sources)
    routed = routed.reshape(EXPERTS, groups * CAP, D)
    quarter = FF // N_TENSOR

    def one_expert(operands):
        expert_rows, w_gate, w_up, w_down = operands
        gate = jnp.dot(expert_rows, w_gate, preferred_element_type=jnp.float32)
        up = jnp.dot(expert_rows, w_up, preferred_element_type=jnp.float32)
        hidden = (jax.nn.silu(gate) * up).astype(jnp.bfloat16)
        summed = jnp.zeros((expert_rows.shape[0], D), jnp.float32)
        for group_num in range(N_TENSOR):
            term = jnp.dot(hidden[:, group_num * quarter:(group_num + 1) * quarter],
                           w_down[group_num * quarter:(group_num + 1) * quarter],
                           preferred_element_type=jnp.float32).astype(jnp.bfloat16)
            term = lax.optimization_barrier(term)
            summed = summed + term.astype(jnp.float32)
        return summed.astype(jnp.bfloat16)

    outputs = lax.map(one_expert, (routed, gate_weight, up_weight, down_weight))
    picked = outputs.reshape(EXPERTS * groups * CAP, D)[target].reshape(TOKENS, TOP, D)
    weights = (2.5 * route_scores / jnp.sum(route_scores, axis=1, keepdims=True)).astype(jnp.bfloat16)
    mixed = jnp.einsum("tk,tkd->td", weights.astype(jnp.float32), picked.astype(jnp.float32))
    return mixed.astype(jnp.bfloat16).reshape(TOKENS, N_DP, D // N_DP)
```

```python
import jax
import jax.numpy as jnp
from jax import lax
from jax.experimental import pallas as pl
from jax.experimental.pallas import tpu as pltpu
from jax.sharding import PartitionSpec as P

MESH = pl.DeviceIdType.MESH
BF16 = jnp.bfloat16
F32 = jnp.float32
TOP = 8
CAP = 8
BLOCK = 16
NZ, NY, NX = 8, 4, 4
HALF = 3584
Q = 896
W2 = 2 * Q
FFQ = 512
ROWS = 512
ORDER = (0, 1, -1, 2, -2, 3, -3, 4)
GROUPS = ((0,), (1, -1), (2, -2), (3, -3), (4,))
START = (0, 1, 3, 5, 7)
NG = len(GROUPS)
N_REMOTE = 128
N_LOCAL = 32


def place_of(offset):
    return ORDER.index((offset + 3) % NZ - 3)


def kernel(
    tokens, ids, scores, wg_hbm, wu_hbm, wd_hbm, out,
    w_gu, w_d, tok, slots, relay, x, own_gu, send_gu, recv_gu, hid, y, xr, zsum, yr, relay2,
    mix, zs, zr, f_own, f_send, f_recv,
    send_sem, recv_sem, local_sem,
):
    e_id, t, d = lax.axis_index("expert"), lax.axis_index("tensor"), lax.axis_index("dp")
    zi, yi = e_id // NY, e_id % NY
    par = t % 2

    def at_z(offset):
        return {"expert": lax.rem(zi + NZ + offset, NZ) * NY + yi, "tensor": t, "dp": d}

    def at_y(offset):
        return {"expert": zi * NY + lax.rem(yi + NY + offset, NY), "tensor": t, "dp": d}

    def at_x(offset, core):
        return {"expert": e_id, "tensor": lax.rem(t + NX + offset, NX), "dp": core}

    remote, local = {}, {}

    def send(key, src, dst, device):
        n = len(remote)
        copy = pltpu.make_async_remote_copy(
            src_ref=src, dst_ref=dst, send_sem=send_sem.at[n], recv_sem=recv_sem.at[n],
            device_id=device, device_id_type=MESH,
        )
        copy.start()
        remote[key] = copy

    def arrived(key):
        remote[key].wait_recv()

    def move(key, src, dst):
        copy = pltpu.make_async_copy(src, dst, local_sem.at[len(local)])
        copy.start()
        local[key] = copy

    def quarter(q):
        return pl.ds(pl.multiple_of(q * Q, 128), Q)

    def half_quarter(half, q):
        return pl.ds(pl.multiple_of(half * HALF + q * Q, 128), Q)

    def block_rows(b):
        return pl.ds(pl.multiple_of(b * BLOCK, BLOCK), BLOCK)

    barrier = pltpu.get_barrier_semaphore()
    peers = [at_z(o) for o in range(1, NZ)] + [at_y(1), at_y(-1), at_x(1, d), at_x(-1, d)]
    peers += [at_x(2, d), at_x(2, 1 - d), at_x(0, 1 - d)]
    for peer in peers:
        pl.semaphore_signal(barrier, inc=1, device_id=peer, device_id_type=MESH)

    move("wg", wg_hbm, w_gu.at[:, pl.ds(0, FFQ)])
    move("wu", wu_hbm, w_gu.at[:, pl.ds(FFQ, FFQ)])
    move("wd", wd_hbm, w_d)
    mine = block_rows(d)
    move("t0", tokens.at[:, half_quarter(d, par)], tok.at[mine, pl.ds(0, Q)])
    move("t1", tokens.at[:, half_quarter(d, par + 2)], tok.at[mine, pl.ds(Q, Q)])

    lane = lax.broadcasted_iota(jnp.int32, (BLOCK, 128), 1)
    chosen, rs = ids[...], scores[...]
    w = (2.5 * rs / jnp.sum(rs, axis=1, keepdims=True)).astype(BF16).astype(F32)
    hot = jnp.zeros((BLOCK, 128), F32)
    weight = jnp.zeros((BLOCK, 128), F32)
    for k in range(TOP):
        ek = chosen[:, k:k + 1]
        hot += jnp.where(ek == lane, 1.0, 0.0)
        weight += jnp.where(ek + 32 == lane, w[:, k:k + 1], 0.0)
    lower = jnp.where(
        lax.broadcasted_iota(jnp.int32, (BLOCK, BLOCK), 0)
        > lax.broadcasted_iota(jnp.int32, (BLOCK, BLOCK), 1), 1.0, 0.0)
    earlier = jnp.dot(lower.astype(BF16), hot.astype(BF16), preferred_element_type=F32)
    table = jnp.where(hot > 0.0, earlier + 1.0, 0.0) + weight
    tok[mine, pl.ds(W2, 128)] = table.astype(BF16)

    pl.semaphore_wait(barrier, len(peers))

    other = at_x(0, 1 - d)
    send("d0", tokens.at[:, half_quarter(1 - d, par)], tok.at[mine, pl.ds(0, Q)], other)
    send("d1", tokens.at[:, half_quarter(1 - d, par + 2)], tok.at[mine, pl.ds(Q, Q)], other)
    send("d2", tok.at[mine, pl.ds(W2, 128)], tok.at[mine, pl.ds(W2, 128)], other)
    for k in ("t0", "t1"):
        local[k].wait()
    for k in ("d0", "d1", "d2"):
        arrived(k)

    def chunk(offset, first=0, count=32):
        return tok.at[pl.ds(32 * place_of(offset) + first, count)]

    def span(g):
        n = len(GROUPS[g])
        return n, 64 * START[g], 16 * n

    def gather_and_place(g):
        n, base, m = span(g)
        if g == 0:
            send(("z", -1), chunk(0), chunk(-1), at_z(1))
            send(("z", 1), chunk(0), chunk(1), at_z(-1))
        elif g < 4:
            for o in GROUPS[g]:
                arrived(("z", o))
            if g < 3:
                send(("z", -g - 1), chunk(-g), chunk(-g - 1), at_z(1))
                send(("z", g + 1), chunk(g), chunk(g + 1), at_z(-1))
            else:
                send(("z", "a"), chunk(-3, 0, 16), chunk(4, 0, 16), at_z(1))
                send(("z", "b"), chunk(3, 16, 16), chunk(4, 16, 16), at_z(-1))
        else:
            arrived(("z", "a"))
            arrived(("z", "b"))
        first = 32 * START[g]
        tab = tok[first:first + 32 * n, W2:]
        col = lax.broadcasted_iota(jnp.int32, (128, 4 * m), 1)
        src = lax.broadcasted_iota(jnp.int32, (128, 4 * m), 0)
        expert = zi * NY + (yi + col // m) % NY
        slot_of = jnp.dot(tab, jnp.where(src == expert, 1.0, 0.0).astype(BF16),
                          preferred_element_type=F32)
        weight_of = jnp.dot(tab, jnp.where(src == expert + 32, 1.0, 0.0).astype(BF16),
                            preferred_element_type=F32)
        c2 = lax.broadcasted_iota(jnp.int32, (32 * n, 4 * m), 1)
        r2 = lax.broadcasted_iota(jnp.int32, (32 * n, 4 * m), 0)
        want = (c2 % CAP + 1).astype(F32)
        hit = (slot_of == want) & ((c2 % m) // CAP == r2 // BLOCK)
        placing = jnp.where(hit, 1.0, 0.0).astype(BF16)
        mix[first:first + 32 * n, 0:4 * m] = jnp.where(hit, weight_of, 0.0).astype(BF16)
        rows = lax.dot_general(
            placing, tok[first:first + 32 * n, 0:W2], (((0,), (0,)), ((), ())),
            preferred_element_type=F32)
        slots[base:base + 4 * m, :] = rows.astype(BF16)
        lo, hi = pl.ds(0, Q), pl.ds(Q, Q)
        qs = (quarter(par), quarter(par + 2))

        def part(j, half):
            return slots.at[pl.ds(base + j * m, m), half]

        def place(c, k):
            return x.at[pl.ds(base + c * m, m), qs[k]]

        rl = pl.ds(16 * START[g], m)
        send(("r", g, 0), part(2, lo), relay.at[0, rl], at_y(1))
        send(("r", g, 1), part(2, hi), relay.at[1, rl], at_y(-1))
        for k, half in enumerate((lo, hi)):
            send(("y1", g, k), part(1, half), place(3, k), at_y(1))
            send(("y3", g, k), part(3, half), place(1, k), at_y(-1))
            move(("y0", g, k), part(0, half), place(0, k))

    def relay_rows(g):
        n, base, m = span(g)
        rl = pl.ds(16 * START[g], m)
        qs = (quarter(par), quarter(par + 2))
        for k, step in ((0, 1), (1, -1)):
            arrived(("r", g, k))
            send(("y2", g, k), relay.at[k, rl], x.at[pl.ds(base + 2 * m, m), qs[k]], at_y(step))

    def swap_halves(g):
        n, base, m = span(g)
        for k in range(2):
            local[("y0", g, k)].wait()
            for kind in ("y1", "y3", "y2"):
                arrived((kind, g, k))
        rows = pl.ds(base, 4 * m)
        for k, step in ((0, 1), (1, -1)):
            view = x.at[rows, quarter(par + 2 * k)]
            send(("x", g, k), view, view, at_x(step, d))

    def gate_up(g):
        n, base, m = span(g)
        if g == 0:
            local["wg"].wait()
            local["wu"].wait()
        for k in range(2):
            arrived(("x", g, k))

        def tile(i, carry):
            cols = pl.ds(pl.multiple_of(i * 256, 256), 256)
            part = jnp.dot(x[base:base + 4 * m, :], w_gu[:, cols], preferred_element_type=F32)
            own_gu[g % 2, 0:4 * m, cols] = part
            send_gu[base:base + 4 * m, cols] = part.astype(BF16)
            return carry

        lax.fori_loop(0, 2 * FFQ // 256, tile, 0)
        rows = pl.ds(base, 4 * m)
        send(("gu", g), send_gu.at[rows], recv_gu.at[rows], at_x(0, 1 - d))

    def down(g):
        n, base, m = span(g)
        if g == 0:
            local["wd"].wait()
        arrived(("gu", g))
        total = own_gu[g % 2, 0:4 * m, :] + recv_gu[base:base + 4 * m, :].astype(F32)
        gate, up = total[:, :FFQ], total[:, FFQ:]
        hid[0:4 * m, :] = (gate / (1.0 + jnp.exp(-gate)) * up).astype(BF16)

        def tile(i, carry):
            cols = pl.ds(pl.multiple_of(i * 512, 512), 512)
            part = jnp.dot(hid[0:4 * m, :], w_d[:, cols], preferred_element_type=F32)
            y[base:base + 4 * m, cols] = part.astype(BF16)
            return carry

        lax.fori_loop(0, HALF // 512, tile, 0)
        rows = pl.ds(base, 4 * m)
        send(("xr", g, 0), y.at[rows, quarter(1 - par)], xr.at[0, rows], at_x(-1, d))
        send(("xr", g, 1), y.at[rows, quarter(3 - par)], xr.at[1, rows], at_x(1, d))

    def add_and_return(g):
        n, base, m = span(g)
        for k in range(2):
            arrived(("xr", g, k))
            mine_y = y[base:base + 4 * m, quarter(par + 2 * k)].astype(F32)
            zsum[base:base + 4 * m, k * Q:(k + 1) * Q] = (
                mine_y + xr[k, base:base + 4 * m, :].astype(F32)).astype(BF16)
        lo, hi = pl.ds(0, Q), pl.ds(Q, Q)
        rl = pl.ds(16 * START[g], m)

        def rows(c):
            return pl.ds(base + c * m, m)

        send(("s", g, 0), zsum.at[rows(2), lo], relay2.at[0, rl], at_y(1))
        send(("s", g, 1), zsum.at[rows(2), hi], relay2.at[1, rl], at_y(-1))
        send(("v1", g), zsum.at[rows(1)], yr.at[rows(3)], at_y(1))
        send(("v3", g), zsum.at[rows(3)], yr.at[rows(1)], at_y(-1))
        move(("v0", g), zsum.at[rows(0)], yr.at[rows(0)])

    def relay_results(g):
        n, base, m = span(g)
        rl = pl.ds(16 * START[g], m)
        rows = pl.ds(base + 2 * m, m)
        for k, step in ((0, 1), (1, -1)):
            arrived(("s", g, k))
            send(("v2", g, k), relay2.at[k, rl], yr.at[rows, pl.ds(k * Q, Q)], at_y(step))

    def combine(g):
        n, base, m = span(g)
        local[("v0", g)].wait()
        for key in (("v1", g), ("v3", g), ("v2", g, 0), ("v2", g, 1)):
            arrived(key)
        first = 32 * START[g]
        part = jnp.dot(mix[first:first + 32 * n, 0:4 * m], yr[base:base + 4 * m, :],
                       preferred_element_type=F32)
        zs[first:first + 32 * n, :] = part.astype(BF16)
        for o in GROUPS[g]:
            if o:
                send(("w", o), zs.at[pl.ds(32 * place_of(o), 32)],
                     zr.at[pl.ds(32 * place_of(-o), 32)], at_z(o))

    stages = (
        (gather_and_place, 0), (gate_up, 2), (relay_rows, 0), (down, 2),
        (add_and_return, 3), (swap_halves, 0), (relay_results, 3), (combine, 4),
    )
    for s in range(NG + 4):
        for stage, lag in stages:
            if 0 <= s - lag < NG:
                stage(s - lag)

    total = zs[0:32, :].astype(F32)
    for o in ORDER[1:]:
        arrived(("w", o))
    for i in range(1, NZ):
        total += zr[32 * i:32 * (i + 1), :].astype(F32)
    low = jnp.broadcast_to(t < 2, (32, Q))
    f_own[...] = jnp.where(low, total[:, :Q], total[:, Q:])
    f_send[0] = f_own[...].astype(BF16)
    f_send[1] = jnp.where(low, total[:, Q:], total[:, :Q]).astype(BF16)
    theirs = block_rows(1 - d)
    send("f0", f_send.at[0, theirs], f_recv.at[0], at_x(0, 1 - d))
    send("f1", f_send.at[1, mine], f_recv.at[1], at_x(2, d))
    send("f2", f_send.at[1, theirs], f_recv.at[2], at_x(2, 1 - d))
    for k in ("f0", "f1", "f2"):
        arrived(k)
    out[d] = (f_own[mine, :] + f_recv[1].astype(F32)).astype(BF16)
    out[1 - d] = (f_recv[0].astype(F32) + f_recv[2].astype(F32)).astype(BF16)
    for copy in remote.values():
        copy.wait_send()


def on_device(tokens, expert_ids, route_scores, gate_weight, up_weight, down_weight):
    vmem = pl.BlockSpec(memory_space=pltpu.VMEM)
    hbm = pl.BlockSpec(memory_space=pl.ANY)
    scratch = [
        pltpu.VMEM((HALF, 2 * FFQ), BF16),
        pltpu.VMEM((FFQ, HALF), BF16),
        pltpu.VMEM((32 * NZ, W2 + 128), BF16),
        pltpu.VMEM((ROWS, W2), BF16),
        pltpu.VMEM((2, 16 * NZ, Q), BF16),
        pltpu.VMEM((ROWS, HALF), BF16),
        pltpu.VMEM((2, 128, 2 * FFQ), F32),
        pltpu.VMEM((ROWS, 2 * FFQ), BF16),
        pltpu.VMEM((ROWS, 2 * FFQ), BF16),
        pltpu.VMEM((128, FFQ), BF16),
        pltpu.VMEM((ROWS, HALF), BF16),
        pltpu.VMEM((2, ROWS, Q), BF16),
        pltpu.VMEM((ROWS, W2), BF16),
        pltpu.VMEM((ROWS, W2), BF16),
        pltpu.VMEM((2, 16 * NZ, Q), BF16),
        pltpu.VMEM((32 * NZ, 128), BF16),
        pltpu.VMEM((32 * NZ, W2), BF16),
        pltpu.VMEM((32 * NZ, W2), BF16),
        pltpu.VMEM((32, Q), F32),
        pltpu.VMEM((2, 32, Q), BF16),
        pltpu.VMEM((3, BLOCK, Q), BF16),
        pltpu.SemaphoreType.DMA((N_REMOTE,)),
        pltpu.SemaphoreType.DMA((N_REMOTE,)),
        pltpu.SemaphoreType.DMA((N_LOCAL,)),
    ]
    out = pl.pallas_call(
        kernel,
        out_shape=jax.ShapeDtypeStruct((2, BLOCK, Q), BF16),
        in_specs=[vmem, vmem, vmem, hbm, hbm, hbm],
        out_specs=vmem,
        scratch_shapes=scratch,
        compiler_params=pltpu.CompilerParams(
            collective_id=0, has_side_effects=True, vmem_limit_bytes=60 * 1024 * 1024
        ),
    )(tokens, expert_ids, route_scores, gate_weight[0], up_weight[0], down_weight[0])
    return out.transpose(1, 0, 2)


def solution(mesh):
    in_specs = (
        P(("expert", "dp"), None),
        P(("expert", "dp"), None),
        P(("expert", "dp"), None),
        P("expert", "dp", "tensor"),
        P("expert", "dp", "tensor"),
        P("expert", "tensor", "dp"),
    )
    out_specs = P(("expert", "dp"), None, "tensor")
    return jax.shard_map(
        on_device, mesh=mesh, in_specs=in_specs, out_specs=out_specs, check_vma=False
    )
```

```python
import jax
import jax.numpy as jnp
from jax import lax
from jax.experimental import pallas as pl
from jax.experimental.pallas import tpu as pltpu
from jax.sharding import PartitionSpec as P

MESH = pl.DeviceIdType.MESH
BF16 = jnp.bfloat16
F32 = jnp.float32
TOP = 8
CAP = 8
BLOCK = 16
NZ, NY, NX = 8, 4, 4
HALF = 3584
Q = 896
W2 = 2 * Q
FFQ = 512
ROWS = 512
ORDER = (0, 1, -1, 2, -2, 3, -3, 4)
GROUPS = ((0,), (1, -1), (2, -2), (3, -3), (4,))
START = (0, 1, 3, 5, 7)
NG = len(GROUPS)
SEQUENCE = (
    "r0", "p0", "r1", "s0", "p1", "r2", "p2", "s1", "g0", "r3", "p3", "s2",
    "r4", "p4", "g1", "s3", "s4", "g2", "g3", "g4", "d4", "d3", "a4", "d2",
    "a3", "d1", "c4", "a2", "d0", "c3", "a1", "c2", "a0", "c1", "c0",
)
N_REMOTE = 128
N_LOCAL = 32


def place_of(offset):
    return ORDER.index((offset + 3) % NZ - 3)


def kernel(
    tokens, ids, scores, wg_hbm, wu_hbm, wd_hbm, out,
    w_gu, w_d, tok, slots, x, own_gu, send_gu, recv_gu, hid, y, xr, zsum, yr,
    mix, zs, zr, f_own, f_send, f_recv,
    send_sem, recv_sem, local_sem,
):
    e_id, t, d = lax.axis_index("expert"), lax.axis_index("tensor"), lax.axis_index("dp")
    zi, yi = e_id // NY, e_id % NY
    par = t % 2

    def at_z(offset):
        return {"expert": lax.rem(zi + NZ + offset, NZ) * NY + yi, "tensor": t, "dp": d}

    def at_y(offset):
        return {"expert": zi * NY + lax.rem(yi + NY + offset, NY), "tensor": t, "dp": d}

    def at_x(offset, core):
        return {"expert": e_id, "tensor": lax.rem(t + NX + offset, NX), "dp": core}

    remote, local = {}, {}

    def send(key, src, dst, device):
        n = len(remote)
        copy = pltpu.make_async_remote_copy(
            src_ref=src, dst_ref=dst, send_sem=send_sem.at[n], recv_sem=recv_sem.at[n],
            device_id=device, device_id_type=MESH,
        )
        copy.start()
        remote[key] = copy

    def arrived(key):
        remote[key].wait_recv()

    def move(key, src, dst):
        copy = pltpu.make_async_copy(src, dst, local_sem.at[len(local)])
        copy.start()
        local[key] = copy

    def quarter(q):
        return pl.ds(pl.multiple_of(q * Q, 128), Q)

    def half_quarter(half, q):
        return pl.ds(pl.multiple_of(half * HALF + q * Q, 128), Q)

    def block_rows(b):
        return pl.ds(pl.multiple_of(b * BLOCK, BLOCK), BLOCK)

    barrier = pltpu.get_barrier_semaphore()
    peers = [at_z(o) for o in range(1, NZ)] + [at_y(1), at_y(2), at_y(-1)]
    peers += [at_x(1, d), at_x(-1, d), at_x(2, d), at_x(2, 1 - d), at_x(0, 1 - d)]
    for peer in peers:
        pl.semaphore_signal(barrier, inc=1, device_id=peer, device_id_type=MESH)

    move("wg", wg_hbm, w_gu.at[:, pl.ds(0, FFQ)])
    move("wu", wu_hbm, w_gu.at[:, pl.ds(FFQ, FFQ)])
    move("wd", wd_hbm, w_d)
    mine = block_rows(d)
    move("t0", tokens.at[:, half_quarter(d, par)], tok.at[mine, pl.ds(0, Q)])
    move("t1", tokens.at[:, half_quarter(d, par + 2)], tok.at[mine, pl.ds(Q, Q)])

    row = lax.broadcasted_iota(jnp.int32, (128, BLOCK), 0)
    chosen, rs = ids[...], scores[...]
    w = (2.5 * rs / jnp.sum(rs, axis=0, keepdims=True)).astype(BF16).astype(F32)
    hot = jnp.zeros((128, BLOCK), F32)
    weight = jnp.zeros((128, BLOCK), F32)
    for k in range(TOP):
        ek = chosen[k:k + 1, :]
        hot += jnp.where(ek == row, 1.0, 0.0)
        weight += jnp.where(ek + 32 == row, w[k:k + 1, :], 0.0)
    before = jnp.where(
        lax.broadcasted_iota(jnp.int32, (BLOCK, BLOCK), 0)
        < lax.broadcasted_iota(jnp.int32, (BLOCK, BLOCK), 1), 1.0, 0.0)
    earlier = jnp.dot(hot.astype(BF16), before.astype(BF16), preferred_element_type=F32)
    turned = jnp.where(hot > 0.0, earlier + 1.0, 0.0) + weight
    eye = jnp.where(
        lax.broadcasted_iota(jnp.int32, (128, 128), 0)
        == lax.broadcasted_iota(jnp.int32, (128, 128), 1), 1.0, 0.0)
    table = lax.dot_general(
        turned.astype(BF16), eye.astype(BF16), (((0,), (0,)), ((), ())),
        preferred_element_type=F32)
    tok[mine, pl.ds(W2, 128)] = table.astype(BF16)

    pl.semaphore_wait(barrier, len(peers))

    other = at_x(0, 1 - d)
    send("d0", tokens.at[:, half_quarter(1 - d, par)], tok.at[mine, pl.ds(0, Q)], other)
    send("d1", tokens.at[:, half_quarter(1 - d, par + 2)], tok.at[mine, pl.ds(Q, Q)], other)
    send("d2", tok.at[mine, pl.ds(W2, 128)], tok.at[mine, pl.ds(W2, 128)], other)
    for k in ("t0", "t1"):
        local[k].wait()
    for k in ("d0", "d1", "d2"):
        arrived(k)

    def chunk(offset, first=0, count=32):
        return tok.at[pl.ds(32 * place_of(offset) + first, count)]

    def span(g):
        n = len(GROUPS[g])
        return n, 64 * START[g], 16 * n

    def ring(g):
        if g == 0:
            send(("z", -1), chunk(0), chunk(-1), at_z(1))
            send(("z", 1), chunk(0), chunk(1), at_z(-1))
        elif g < 4:
            for o in GROUPS[g]:
                arrived(("z", o))
            if g < 3:
                send(("z", -g - 1), chunk(-g), chunk(-g - 1), at_z(1))
                send(("z", g + 1), chunk(g), chunk(g + 1), at_z(-1))
            else:
                send(("z", "a"), chunk(-3, 0, 16), chunk(4, 0, 16), at_z(1))
                send(("z", "b"), chunk(3, 16, 16), chunk(4, 16, 16), at_z(-1))
        else:
            arrived(("z", "a"))
            arrived(("z", "b"))

    def place_rows(g):
        n, base, m = span(g)
        first = 32 * START[g]
        tab = tok[first:first + 32 * n, W2:]
        col = lax.broadcasted_iota(jnp.int32, (128, 4 * m), 1)
        src = lax.broadcasted_iota(jnp.int32, (128, 4 * m), 0)
        expert = zi * NY + (yi + col // m) % NY
        slot_of = jnp.dot(tab, jnp.where(src == expert, 1.0, 0.0).astype(BF16),
                          preferred_element_type=F32)
        weight_of = jnp.dot(tab, jnp.where(src == expert + 32, 1.0, 0.0).astype(BF16),
                            preferred_element_type=F32)
        c2 = lax.broadcasted_iota(jnp.int32, (32 * n, 4 * m), 1)
        r2 = lax.broadcasted_iota(jnp.int32, (32 * n, 4 * m), 0)
        want = (c2 % CAP + 1).astype(F32)
        hit = (slot_of == want) & ((c2 % m) // CAP == r2 // BLOCK)
        placing = jnp.where(hit, 1.0, 0.0).astype(BF16)
        mix[first:first + 32 * n, 0:4 * m] = jnp.where(hit, weight_of, 0.0).astype(BF16)
        rows = lax.dot_general(
            placing, tok[first:first + 32 * n, 0:W2], (((0,), (0,)), ((), ())),
            preferred_element_type=F32)
        slots[base:base + 4 * m, :] = rows.astype(BF16)
        lo, hi = pl.ds(0, Q), pl.ds(Q, Q)
        qs = (quarter(par), quarter(par + 2))

        def part(j, half):
            return slots.at[pl.ds(base + j * m, m), half]

        def place(c, k):
            return x.at[pl.ds(base + c * m, m), qs[k]]

        for k, half in enumerate((lo, hi)):
            send(("y2", g, k), part(2, half), place(2, k), at_y(2))
            send(("y1", g, k), part(1, half), place(3, k), at_y(1))
            send(("y3", g, k), part(3, half), place(1, k), at_y(-1))
            move(("y0", g, k), part(0, half), place(0, k))

    def swap_halves(g):
        n, base, m = span(g)
        for k in range(2):
            local[("y0", g, k)].wait()
            for kind in ("y1", "y3", "y2"):
                arrived((kind, g, k))
        rows = pl.ds(base, 4 * m)
        for k, step in ((0, 1), (1, -1)):
            view = x.at[rows, quarter(par + 2 * k)]
            send(("x", g, k), view, view, at_x(step, d))

    def gate_up(g):
        n, base, m = span(g)
        if g == 0:
            local["wg"].wait()
            local["wu"].wait()
            local["wd"].wait()
        for k in range(2):
            arrived(("x", g, k))

        def tile(i, carry):
            cols = pl.ds(pl.multiple_of(i * 256, 256), 256)
            part = jnp.dot(x[base:base + 4 * m, :], w_gu[:, cols], preferred_element_type=F32)
            own_gu[g, 0:4 * m, cols] = part
            send_gu[base:base + 4 * m, cols] = part.astype(BF16)
            return carry

        lax.fori_loop(0, 2 * FFQ // 256, tile, 0)
        rows = pl.ds(base, 4 * m)
        send(("gu", g), send_gu.at[rows], recv_gu.at[rows], at_x(0, 1 - d))

    def down(g):
        n, base, m = span(g)
        arrived(("gu", g))
        total = own_gu[g, 0:4 * m, :] + recv_gu[base:base + 4 * m, :].astype(F32)
        gate, up = total[:, :FFQ], total[:, FFQ:]
        hid[0:4 * m, :] = (gate / (1.0 + jnp.exp(-gate)) * up).astype(BF16)

        def tile(i, carry):
            cols = pl.ds(pl.multiple_of(i * 512, 512), 512)
            part = jnp.dot(hid[0:4 * m, :], w_d[:, cols], preferred_element_type=F32)
            y[base:base + 4 * m, cols] = part.astype(BF16)
            return carry

        lax.fori_loop(0, HALF // 512, tile, 0)
        rows = pl.ds(base, 4 * m)
        send(("xr", g, 0), y.at[rows, quarter(1 - par)], xr.at[0, rows], at_x(-1, d))
        send(("xr", g, 1), y.at[rows, quarter(3 - par)], xr.at[1, rows], at_x(1, d))

    def add_and_return(g):
        n, base, m = span(g)
        for k in range(2):
            arrived(("xr", g, k))
            mine_y = y[base:base + 4 * m, quarter(par + 2 * k)].astype(F32)
            zsum[base:base + 4 * m, k * Q:(k + 1) * Q] = (
                mine_y + xr[k, base:base + 4 * m, :].astype(F32)).astype(BF16)

        def rows(c):
            return pl.ds(base + c * m, m)

        send(("v2", g), zsum.at[rows(2)], yr.at[rows(2)], at_y(2))
        send(("v1", g), zsum.at[rows(1)], yr.at[rows(3)], at_y(1))
        send(("v3", g), zsum.at[rows(3)], yr.at[rows(1)], at_y(-1))
        move(("v0", g), zsum.at[rows(0)], yr.at[rows(0)])

    def combine(g):
        n, base, m = span(g)
        local[("v0", g)].wait()
        for key in (("v1", g), ("v3", g), ("v2", g)):
            arrived(key)
        first = 32 * START[g]
        part = jnp.dot(mix[first:first + 32 * n, 0:4 * m], yr[base:base + 4 * m, :],
                       preferred_element_type=F32)
        zs[first:first + 32 * n, :] = part.astype(BF16)
        for o in GROUPS[g]:
            if o:
                send(("w", o), zs.at[pl.ds(32 * place_of(o), 32)],
                     zr.at[pl.ds(32 * place_of(-o), 32)], at_z(o))

    stages = {
        "r": ring, "p": place_rows, "s": swap_halves, "g": gate_up,
        "d": down, "a": add_and_return, "c": combine,
    }
    for step in SEQUENCE:
        stages[step[0]](int(step[1]))

    total = zs[0:32, :].astype(F32)
    for o in ORDER[1:]:
        arrived(("w", o))
    for i in range(1, NZ):
        total += zr[32 * i:32 * (i + 1), :].astype(F32)
    low = jnp.broadcast_to(t < 2, (32, Q))
    f_own[...] = jnp.where(low, total[:, :Q], total[:, Q:])
    f_send[0] = f_own[...].astype(BF16)
    f_send[1] = jnp.where(low, total[:, Q:], total[:, :Q]).astype(BF16)
    theirs = block_rows(1 - d)
    send("f0", f_send.at[0, theirs], f_recv.at[0], at_x(0, 1 - d))
    send("f1", f_send.at[1, mine], f_recv.at[1], at_x(2, d))
    send("f2", f_send.at[1, theirs], f_recv.at[2], at_x(2, 1 - d))
    for k in ("f0", "f1", "f2"):
        arrived(k)
    out[d] = (f_own[mine, :] + f_recv[1].astype(F32)).astype(BF16)
    out[1 - d] = (f_recv[0].astype(F32) + f_recv[2].astype(F32)).astype(BF16)
    for copy in remote.values():
        copy.wait_send()


def on_device(tokens, expert_ids, route_scores, gate_weight, up_weight, down_weight):
    vmem = pl.BlockSpec(memory_space=pltpu.VMEM)
    hbm = pl.BlockSpec(memory_space=pl.ANY)
    scratch = [
        pltpu.VMEM((HALF, 2 * FFQ), BF16),
        pltpu.VMEM((FFQ, HALF), BF16),
        pltpu.VMEM((32 * NZ, W2 + 128), BF16),
        pltpu.VMEM((ROWS, W2), BF16),
        pltpu.VMEM((ROWS, HALF), BF16),
        pltpu.VMEM((NG, 128, 2 * FFQ), F32),
        pltpu.VMEM((ROWS, 2 * FFQ), BF16),
        pltpu.VMEM((ROWS, 2 * FFQ), BF16),
        pltpu.VMEM((128, FFQ), BF16),
        pltpu.VMEM((ROWS, HALF), BF16),
        pltpu.VMEM((2, ROWS, Q), BF16),
        pltpu.VMEM((ROWS, W2), BF16),
        pltpu.VMEM((ROWS, W2), BF16),
        pltpu.VMEM((32 * NZ, 128), BF16),
        pltpu.VMEM((32 * NZ, W2), BF16),
        pltpu.VMEM((32 * NZ, W2), BF16),
        pltpu.VMEM((32, Q), F32),
        pltpu.VMEM((2, 32, Q), BF16),
        pltpu.VMEM((3, BLOCK, Q), BF16),
        pltpu.SemaphoreType.DMA((N_REMOTE,)),
        pltpu.SemaphoreType.DMA((N_REMOTE,)),
        pltpu.SemaphoreType.DMA((N_LOCAL,)),
    ]
    out = pl.pallas_call(
        kernel,
        out_shape=jax.ShapeDtypeStruct((2, BLOCK, Q), BF16),
        in_specs=[vmem, vmem, vmem, hbm, hbm, hbm],
        out_specs=vmem,
        scratch_shapes=scratch,
        compiler_params=pltpu.CompilerParams(
            collective_id=0, has_side_effects=True, vmem_limit_bytes=60 * 1024 * 1024
        ),
    )(tokens, expert_ids.T, route_scores.T, gate_weight[0], up_weight[0], down_weight[0])
    return out.transpose(1, 0, 2)


def solution(mesh):
    in_specs = (
        P(("expert", "dp"), None),
        P(("expert", "dp"), None),
        P(("expert", "dp"), None),
        P("expert", "dp", "tensor"),
        P("expert", "dp", "tensor"),
        P("expert", "tensor", "dp"),
    )
    out_specs = P(("expert", "dp"), None, "tensor")
    return jax.shard_map(
        on_device, mesh=mesh, in_specs=in_specs, out_specs=out_specs, check_vma=False
    )
```

```python
import jax
import jax.numpy as jnp
from jax import lax
from jax.experimental import pallas as pl
from jax.experimental.pallas import tpu as pltpu
from jax.sharding import PartitionSpec as P

MESH = pl.DeviceIdType.MESH
BF16 = jnp.bfloat16
F32 = jnp.float32
TOP = 8
CAP = 8
BLOCK = 16
NZ, NY, NX = 8, 4, 4
HALF = 3584
Q = 896
W2 = 2 * Q
FFQ = 512
ROWS = 512
ORDER = (0, 1, -1, 2, -2, 3, -3, 4)
GROUPS = ((0,), (1, -1), (2, -2), (3, -3), (4,))
START = (0, 1, 3, 5, 7)
NG = len(GROUPS)
SEQUENCE = (
    "r0", "p0", "r1", "s0", "p1", "r2", "p2", "s1", "g0", "r3", "p3", "s2",
    "r4", "p4", "g1", "s3", "g2", "s4", "d2", "g3", "g4", "a2", "d3", "d4",
    "a3", "c2", "a4", "d1", "c3", "d0", "c4", "a1", "a0", "c1", "c0",
)
N_REMOTE = 128
N_LOCAL = 32


def place_of(offset):
    return ORDER.index((offset + 3) % NZ - 3)


def kernel(
    tokens, ids, scores, wg_hbm, wu_hbm, wd_hbm, out,
    w_gu, w_d, tok, slots, x, own_gu, send_gu, recv_gu, hid, y, xr, zsum, yr,
    mix, zs, zr, f_own, f_send, f_recv,
    send_sem, recv_sem, local_sem,
):
    e_id, t, d = lax.axis_index("expert"), lax.axis_index("tensor"), lax.axis_index("dp")
    zi, yi = e_id // NY, e_id % NY
    par = t % 2

    def at_z(offset):
        return {"expert": lax.rem(zi + NZ + offset, NZ) * NY + yi, "tensor": t, "dp": d}

    def at_y(offset):
        return {"expert": zi * NY + lax.rem(yi + NY + offset, NY), "tensor": t, "dp": d}

    def at_x(offset, core):
        return {"expert": e_id, "tensor": lax.rem(t + NX + offset, NX), "dp": core}

    remote, local = {}, {}

    def send(key, src, dst, device):
        n = len(remote)
        copy = pltpu.make_async_remote_copy(
            src_ref=src, dst_ref=dst, send_sem=send_sem.at[n], recv_sem=recv_sem.at[n],
            device_id=device, device_id_type=MESH,
        )
        copy.start()
        remote[key] = copy

    def arrived(key):
        remote[key].wait_recv()

    def move(key, src, dst):
        copy = pltpu.make_async_copy(src, dst, local_sem.at[len(local)])
        copy.start()
        local[key] = copy

    def quarter(q):
        return pl.ds(pl.multiple_of(q * Q, 128), Q)

    def half_quarter(half, q):
        return pl.ds(pl.multiple_of(half * HALF + q * Q, 128), Q)

    def block_rows(b):
        return pl.ds(pl.multiple_of(b * BLOCK, BLOCK), BLOCK)

    barrier = pltpu.get_barrier_semaphore()
    peers = [at_z(o) for o in range(1, NZ)] + [at_y(1), at_y(2), at_y(-1)]
    peers += [at_x(1, d), at_x(-1, d), at_x(2, d), at_x(2, 1 - d), at_x(0, 1 - d)]
    for peer in peers:
        pl.semaphore_signal(barrier, inc=1, device_id=peer, device_id_type=MESH)

    move("wg", wg_hbm, w_gu.at[:, pl.ds(0, FFQ)])
    move("wu", wu_hbm, w_gu.at[:, pl.ds(FFQ, FFQ)])
    move("wd", wd_hbm, w_d)
    mine = block_rows(d)
    move("t0", tokens.at[:, half_quarter(d, par)], tok.at[mine, pl.ds(0, Q)])
    move("t1", tokens.at[:, half_quarter(d, par + 2)], tok.at[mine, pl.ds(Q, Q)])

    row = lax.broadcasted_iota(jnp.int32, (128, BLOCK), 0)
    chosen, rs = ids[...], scores[...]
    w = (2.5 * rs / jnp.sum(rs, axis=0, keepdims=True)).astype(BF16).astype(F32)
    hot = jnp.zeros((128, BLOCK), F32)
    weight = jnp.zeros((128, BLOCK), F32)
    for k in range(TOP):
        ek = chosen[k:k + 1, :]
        hot += jnp.where(ek == row, 1.0, 0.0)
        weight += jnp.where(ek + 32 == row, w[k:k + 1, :], 0.0)
    before = jnp.where(
        lax.broadcasted_iota(jnp.int32, (BLOCK, BLOCK), 0)
        < lax.broadcasted_iota(jnp.int32, (BLOCK, BLOCK), 1), 1.0, 0.0)
    earlier = jnp.dot(hot.astype(BF16), before.astype(BF16), preferred_element_type=F32)
    turned = jnp.where(hot > 0.0, earlier + 1.0, 0.0) + weight
    eye = jnp.where(
        lax.broadcasted_iota(jnp.int32, (128, 128), 0)
        == lax.broadcasted_iota(jnp.int32, (128, 128), 1), 1.0, 0.0)
    table = lax.dot_general(
        turned.astype(BF16), eye.astype(BF16), (((0,), (0,)), ((), ())),
        preferred_element_type=F32)
    tok[mine, pl.ds(W2, 128)] = table.astype(BF16)

    pl.semaphore_wait(barrier, len(peers))

    other = at_x(0, 1 - d)
    send("d0", tokens.at[:, half_quarter(1 - d, par)], tok.at[mine, pl.ds(0, Q)], other)
    send("d1", tokens.at[:, half_quarter(1 - d, par + 2)], tok.at[mine, pl.ds(Q, Q)], other)
    send("d2", tok.at[mine, pl.ds(W2, 128)], tok.at[mine, pl.ds(W2, 128)], other)
    for k in ("t0", "t1"):
        local[k].wait()
    for k in ("d0", "d1", "d2"):
        arrived(k)

    def chunk(offset, first=0, count=32):
        return tok.at[pl.ds(32 * place_of(offset) + first, count)]

    def span(g):
        n = len(GROUPS[g])
        return n, 64 * START[g], 16 * n

    def ring(g):
        if g == 0:
            send(("z", -1), chunk(0), chunk(-1), at_z(1))
            send(("z", 1), chunk(0), chunk(1), at_z(-1))
        elif g < 4:
            for o in GROUPS[g]:
                arrived(("z", o))
            if g < 3:
                send(("z", -g - 1), chunk(-g), chunk(-g - 1), at_z(1))
                send(("z", g + 1), chunk(g), chunk(g + 1), at_z(-1))
            else:
                send(("z", "a"), chunk(-3, 0, 16), chunk(4, 0, 16), at_z(1))
                send(("z", "b"), chunk(3, 16, 16), chunk(4, 16, 16), at_z(-1))
        else:
            arrived(("z", "a"))
            arrived(("z", "b"))

    def place_rows(g):
        n, base, m = span(g)
        first = 32 * START[g]
        tab = tok[first:first + 32 * n, W2:]
        col = lax.broadcasted_iota(jnp.int32, (128, 4 * m), 1)
        src = lax.broadcasted_iota(jnp.int32, (128, 4 * m), 0)
        expert = zi * NY + (yi + col // m) % NY
        slot_of = jnp.dot(tab, jnp.where(src == expert, 1.0, 0.0).astype(BF16),
                          preferred_element_type=F32)
        weight_of = jnp.dot(tab, jnp.where(src == expert + 32, 1.0, 0.0).astype(BF16),
                            preferred_element_type=F32)
        c2 = lax.broadcasted_iota(jnp.int32, (32 * n, 4 * m), 1)
        r2 = lax.broadcasted_iota(jnp.int32, (32 * n, 4 * m), 0)
        want = (c2 % CAP + 1).astype(F32)
        hit = (slot_of == want) & ((c2 % m) // CAP == r2 // BLOCK)
        placing = jnp.where(hit, 1.0, 0.0).astype(BF16)
        mix[first:first + 32 * n, 0:4 * m] = jnp.where(hit, weight_of, 0.0).astype(BF16)
        rows = lax.dot_general(
            placing, tok[first:first + 32 * n, 0:W2], (((0,), (0,)), ((), ())),
            preferred_element_type=F32)
        slots[base:base + 4 * m, :] = rows.astype(BF16)
        lo, hi = pl.ds(0, Q), pl.ds(Q, Q)
        qs = (quarter(par), quarter(par + 2))

        def part(j, half):
            return slots.at[pl.ds(base + j * m, m), half]

        def place(c, k):
            return x.at[pl.ds(base + c * m, m), qs[k]]

        for k, half in enumerate((lo, hi)):
            send(("y2", g, k), part(2, half), place(2, k), at_y(2))
            send(("y1", g, k), part(1, half), place(3, k), at_y(1))
            send(("y3", g, k), part(3, half), place(1, k), at_y(-1))
            move(("y0", g, k), part(0, half), place(0, k))

    def swap_halves(g):
        n, base, m = span(g)
        for k in range(2):
            local[("y0", g, k)].wait()
            for kind in ("y1", "y3", "y2"):
                arrived((kind, g, k))
        rows = pl.ds(base, 4 * m)
        for k, step in ((0, 1), (1, -1)):
            view = x.at[rows, quarter(par + 2 * k)]
            send(("x", g, k), view, view, at_x(step, d))

    def gate_up(g):
        n, base, m = span(g)
        if g == 0:
            local["wg"].wait()
            local["wu"].wait()
            local["wd"].wait()
        for k in range(2):
            arrived(("x", g, k))

        def tile(i, carry):
            cols = pl.ds(pl.multiple_of(i * 256, 256), 256)
            part = jnp.dot(x[base:base + 4 * m, :], w_gu[:, cols], preferred_element_type=F32)
            own_gu[g, 0:4 * m, cols] = part
            send_gu[base:base + 4 * m, cols] = part.astype(BF16)
            return carry

        lax.fori_loop(0, 2 * FFQ // 256, tile, 0)
        rows = pl.ds(base, 4 * m)
        send(("gu", g), send_gu.at[rows], recv_gu.at[rows], at_x(0, 1 - d))

    def down(g):
        n, base, m = span(g)
        arrived(("gu", g))
        total = own_gu[g, 0:4 * m, :] + recv_gu[base:base + 4 * m, :].astype(F32)
        gate, up = total[:, :FFQ], total[:, FFQ:]
        hid[0:4 * m, :] = (gate / (1.0 + jnp.exp(-gate)) * up).astype(BF16)

        def tile(i, carry):
            cols = pl.ds(pl.multiple_of(i * 512, 512), 512)
            part = jnp.dot(hid[0:4 * m, :], w_d[:, cols], preferred_element_type=F32)
            y[base:base + 4 * m, cols] = part.astype(BF16)
            return carry

        lax.fori_loop(0, HALF // 512, tile, 0)
        rows = pl.ds(base, 4 * m)
        send(("xr", g, 0), y.at[rows, quarter(1 - par)], xr.at[0, rows], at_x(-1, d))
        send(("xr", g, 1), y.at[rows, quarter(3 - par)], xr.at[1, rows], at_x(1, d))

    def add_and_return(g):
        n, base, m = span(g)
        for k in range(2):
            arrived(("xr", g, k))
            mine_y = y[base:base + 4 * m, quarter(par + 2 * k)].astype(F32)
            zsum[base:base + 4 * m, k * Q:(k + 1) * Q] = (
                mine_y + xr[k, base:base + 4 * m, :].astype(F32)).astype(BF16)

        def rows(c):
            return pl.ds(base + c * m, m)

        send(("v2", g), zsum.at[rows(2)], yr.at[rows(2)], at_y(2))
        send(("v1", g), zsum.at[rows(1)], yr.at[rows(3)], at_y(1))
        send(("v3", g), zsum.at[rows(3)], yr.at[rows(1)], at_y(-1))
        move(("v0", g), zsum.at[rows(0)], yr.at[rows(0)])

    def combine(g):
        n, base, m = span(g)
        local[("v0", g)].wait()
        for key in (("v1", g), ("v3", g), ("v2", g)):
            arrived(key)
        first = 32 * START[g]
        part = jnp.dot(mix[first:first + 32 * n, 0:4 * m], yr[base:base + 4 * m, :],
                       preferred_element_type=F32)
        zs[first:first + 32 * n, :] = part.astype(BF16)
        for o in GROUPS[g]:
            if o:
                send(("w", o), zs.at[pl.ds(32 * place_of(o), 32)],
                     zr.at[pl.ds(32 * place_of(-o), 32)], at_z(o))

    stages = {
        "r": ring, "p": place_rows, "s": swap_halves, "g": gate_up,
        "d": down, "a": add_and_return, "c": combine,
    }
    for step in SEQUENCE:
        stages[step[0]](int(step[1]))

    total = zs[0:32, :].astype(F32)
    for o in ORDER[1:]:
        arrived(("w", o))
    for i in range(1, NZ):
        total += zr[32 * i:32 * (i + 1), :].astype(F32)
    low = jnp.broadcast_to(t < 2, (32, Q))
    f_own[...] = jnp.where(low, total[:, :Q], total[:, Q:])
    f_send[0] = f_own[...].astype(BF16)
    f_send[1] = jnp.where(low, total[:, Q:], total[:, :Q]).astype(BF16)
    theirs = block_rows(1 - d)
    send("f0", f_send.at[0, theirs], f_recv.at[0], at_x(0, 1 - d))
    send("f1", f_send.at[1, mine], f_recv.at[1], at_x(2, d))
    send("f2", f_send.at[1, theirs], f_recv.at[2], at_x(2, 1 - d))
    for k in ("f0", "f1", "f2"):
        arrived(k)
    out[d] = (f_own[mine, :] + f_recv[1].astype(F32)).astype(BF16)
    out[1 - d] = (f_recv[0].astype(F32) + f_recv[2].astype(F32)).astype(BF16)
    for copy in remote.values():
        copy.wait_send()


def on_device(tokens, expert_ids, route_scores, gate_weight, up_weight, down_weight):
    vmem = pl.BlockSpec(memory_space=pltpu.VMEM)
    hbm = pl.BlockSpec(memory_space=pl.ANY)
    scratch = [
        pltpu.VMEM((HALF, 2 * FFQ), BF16),
        pltpu.VMEM((FFQ, HALF), BF16),
        pltpu.VMEM((32 * NZ, W2 + 128), BF16),
        pltpu.VMEM((ROWS, W2), BF16),
        pltpu.VMEM((ROWS, HALF), BF16),
        pltpu.VMEM((NG, 128, 2 * FFQ), F32),
        pltpu.VMEM((ROWS, 2 * FFQ), BF16),
        pltpu.VMEM((ROWS, 2 * FFQ), BF16),
        pltpu.VMEM((128, FFQ), BF16),
        pltpu.VMEM((ROWS, HALF), BF16),
        pltpu.VMEM((2, ROWS, Q), BF16),
        pltpu.VMEM((ROWS, W2), BF16),
        pltpu.VMEM((ROWS, W2), BF16),
        pltpu.VMEM((32 * NZ, 128), BF16),
        pltpu.VMEM((32 * NZ, W2), BF16),
        pltpu.VMEM((32 * NZ, W2), BF16),
        pltpu.VMEM((32, Q), F32),
        pltpu.VMEM((2, 32, Q), BF16),
        pltpu.VMEM((3, BLOCK, Q), BF16),
        pltpu.SemaphoreType.DMA((N_REMOTE,)),
        pltpu.SemaphoreType.DMA((N_REMOTE,)),
        pltpu.SemaphoreType.DMA((N_LOCAL,)),
    ]
    out = pl.pallas_call(
        kernel,
        out_shape=jax.ShapeDtypeStruct((2, BLOCK, Q), BF16),
        in_specs=[vmem, vmem, vmem, hbm, hbm, hbm],
        out_specs=vmem,
        scratch_shapes=scratch,
        compiler_params=pltpu.CompilerParams(
            collective_id=0, has_side_effects=True, vmem_limit_bytes=60 * 1024 * 1024
        ),
    )(tokens, expert_ids.T, route_scores.T, gate_weight[0], up_weight[0], down_weight[0])
    return out.transpose(1, 0, 2)


def solution(mesh):
    in_specs = (
        P(("expert", "dp"), None),
        P(("expert", "dp"), None),
        P(("expert", "dp"), None),
        P("expert", "dp", "tensor"),
        P("expert", "dp", "tensor"),
        P("expert", "tensor", "dp"),
    )
    out_specs = P(("expert", "dp"), None, "tensor")
    return jax.shard_map(
        on_device, mesh=mesh, in_specs=in_specs, out_specs=out_specs, check_vma=False
    )
```
